256 devices in a mesh: occ: 8 (over y_lo, x), vir: 32 (over y_hi, z, core).
Axes of the slice: x: 4, y: 4 (y_hi: 2, y_lo: 2; y = y_hi * 2 + y_lo), z: 8, core: 2. Of those that a mesh axis runs over, the one named last changes fastest.
Arguments:
- factors: bfloat16 [256, 1024, 2048], P(None, 'vir', 'occ'), may hold values from -0.125 to 0.125
- e_occ: float32 [256], replicated, may hold values from -2 to -0.3
- e_vir: float32 [1024], replicated, may hold values from 0.1 to 3
- i_sub: int32 [3], replicated, may hold values from 0 to 1
- j_row: int32 [3], replicated, may hold values from 0 to 255
Outputs:
- density: float32 [256, 1024, 2048], P(None, 'vir', 'occ')
The draws below stay inside these ranges and needn't reach their ends.
All inputs are finite; a program needn't handle non-finite values.
Results may differ from the reference program's by a relative error of at most 0.0022.
Values may be sent and summed in bfloat16 or wider, within the bound.
A program may use at most 128 MiB of HBM per device.

```python
import jax
import jax.numpy as jnp
from jax import lax

NOCC = 256
NVIR = 1024
NAUX = 2048
IBK = 16
STEPS = 3
SUBS = 2
N_OCC = 8


def steps_of(key, shape, split, smallest, high):
    factor_of = 1.0
    for dim, shards_of in split:
        steps = jax.random.uniform(jax.random.fold_in(jax.random.fold_in(key, 6), dim), (shards_of,), jnp.float32, smallest / len(split), high / len(split))
        factor_of = factor_of * jnp.repeat(jnp.exp(steps), shape[dim] // shards_of).reshape((-1,) + (1,) * (len(shape) - 1 - dim))
    return factor_of


def bell_draw(stream_key, dims, scale, reach, shards=(), dtype=jnp.bfloat16):
    array = scale * jax.random.normal(stream_key, dims, jnp.float32)
    if shards:
        array = array * steps_of(stream_key, dims, shards, -0.22, 0.18)
    return jnp.clip(array, -reach, reach).astype(dtype)


def setup_inputs(seed: int = 0) -> dict:
    streams_of = jax.random.split(jax.random.key(seed), 6)
    return {
        "factors": bell_draw(streams_of[0], (NOCC, NVIR, NAUX), NAUX ** -0.5, 0.125, ((1, 32), (2, 8))),
        "e_occ": jnp.clip(jax.random.uniform(streams_of[1], (NOCC,), jnp.float32, -2.0, -0.3), -2.0, -0.3),
        "e_vir": jnp.clip(jax.random.uniform(streams_of[2], (NVIR,), jnp.float32, 0.1, 3.0), 0.1, 3.0),
        "i_sub": jax.random.randint(streams_of[3], (STEPS,), 0, SUBS).astype(jnp.int32),
        "j_row": jax.random.randint(streams_of[4], (STEPS,), 0, NOCC).astype(jnp.int32),
    }


def reference(factors, e_occ, e_vir, i_sub, j_row):
    owned = NOCC // N_OCC
    density = jnp.zeros((NOCC, NVIR, NAUX), jnp.float32)
    for step_index in range(STEPS):
        j_index = j_row[step_index]
        pair_slab = lax.dynamic_index_in_dim(factors, j_index, 0, keepdims=False).astype(jnp.float32)
        energy_pair = e_occ[j_index]
        offset = i_sub[step_index] * IBK

        def owner_step(owner, density):
            first_row = (owner * owned + offset).astype(jnp.int32)
            row_block = lax.dynamic_slice_in_dim(factors, first_row, IBK, 0).astype(jnp.float32)
            energy_rows = lax.dynamic_slice_in_dim(e_occ, first_row, IBK, 0)
            integrals = jnp.einsum("iap,bp->iab", row_block, pair_slab)
            denominator = e_vir[None, :, None] + e_vir[None, None, :] - energy_rows[:, None, None] - energy_pair
            amplitude = (-integrals / denominator).astype(jnp.bfloat16)
            contribution = jnp.einsum("iab,bp->iap", amplitude.astype(jnp.float32), pair_slab)
            previous = lax.dynamic_slice_in_dim(density, first_row, IBK, 0)
            return lax.dynamic_update_slice_in_dim(density, previous + contribution, first_row, 0)

        density = lax.fori_loop(0, N_OCC, owner_step, density)
    return density
```

```python
import jax
import jax.numpy as jnp
from jax import lax
from jax.experimental import pallas as pl
from jax.experimental.pallas import tpu as pltpu
from jax.sharding import PartitionSpec as P

MESH = pl.DeviceIdType.MESH
F32 = jnp.float32
BF16 = jnp.bfloat16

STEPS = 3
IBK = 16
OCC = 8
VIR = 32
AB = 32
PB = 256
CHUNKS = 2
KB = IBK // CHUNKS
M = KB * AB
NB = 256
JB = VIR * AB // NB
VB = NB // AB


def rotate(index, shift, size):
    return lax.rem(index + (shift + size), size)


def kernel(
    i_sub, j_row, e_occ, e_vir, factors, own_pair, out,
    pair, rows0, rows1, er, amp, acc, snd0, snd1,
    in_s, in_r, gat_s, gat_r, z_s, z_r, f_s, f_r, p_s, p_r, o_s, o_r, loc,
):
    o, v = lax.axis_index("occ"), lax.axis_index("vir")
    yl, x = o // 4, lax.rem(o, 4)
    yh, z, core = v // 16, lax.rem(v // 2, 8), lax.rem(v, 2)
    rows, snd = (rows0, rows1), (snd0, snd1)

    def occ_at(d):
        return lax.rem(yl + d // 4, 2) * 4 + lax.rem(x + lax.rem(d, 4), 4)

    def occ_from(d):
        return lax.rem(yl + d // 4, 2) * 4 + lax.rem(x + 4 - lax.rem(d, 4), 4)

    def block_at(side, dz):
        high = 1 - yh if side else yh
        return high * 16 + rotate(z, dz, 8) * 2 + core

    far = ((1 - yl) * 4 + x, (1 - yh) * 16 + z * 2 + core)
    mate = (o, v + 1 - 2 * core)
    up = (o, block_at(0, 1))
    down = (o, block_at(0, -1))

    barrier = pltpu.get_barrier_semaphore()
    for d in range(1, OCC):
        pl.semaphore_signal(barrier, inc=1, device_id=(occ_at(d), v), device_id_type=MESH)
    for device in (far, mate, up, down):
        pl.semaphore_signal(barrier, inc=1, device_id=device, device_id_type=MESH)
    pl.semaphore_wait(barrier, OCC + 3)

    sends = []

    def send(src, dst, ssem, rsem, device):
        copy = pltpu.make_async_remote_copy(
            src_ref=src, dst_ref=dst, send_sem=ssem, recv_sem=rsem, device_id=device, device_id_type=MESH
        )
        copy.start()
        sends.append(copy)

    def arrived(ref, rsem):
        pltpu.make_async_copy(ref, ref, rsem).wait()

    own_copies = [pltpu.make_async_copy(own_pair, pair.at[:, v, o], loc.at[0])]
    own_copies += [pltpu.make_async_copy(factors.at[o, :, pl.ds(c * KB, KB)], rows[c].at[o], loc.at[1 + c]) for c in range(CHUNKS)]
    for copy in own_copies:
        copy.start()

    order = (1, 3, 4, 5, 7, 2, 6)
    for d in order:
        send(own_pair, pair.at[:, v, o], gat_s.at[d], gat_r.at[d], (occ_at(d), v))
    for c in range(CHUNKS):
        for u in range(2):
            for d in order:
                r = occ_at(d)
                send(factors.at[r, u, pl.ds(c * KB, KB)], rows[c].at[o, u], in_s.at[c, u, d], in_r.at[c, u, d], (r, v))

    lanes = lax.broadcasted_iota(jnp.int32, (AB, 128), 1)
    subl = lax.broadcasted_iota(jnp.int32, (AB, 128), 0)
    mine = e_vir[pl.ds(v // 4, 1), :]
    own_e = jnp.sum(jnp.where(lanes == subl + lax.rem(v, 4) * AB, mine, 0.0), axis=1, keepdims=True)
    for s in range(STEPS):
        e_pair = e_occ[j_row[s]]
        first = o * 32 + i_sub[s] * IBK
        for k in range(IBK):
            er[s, k * AB : (k + 1) * AB, :] = jnp.broadcast_to(own_e - e_occ[first + k] - e_pair, (AB, 128))

    streams = ((0, 0), (0, 1), (1, 0), (2, 0))
    half = {1: pl.ds(0, 4), -1: pl.ds(4, 4)}

    def view(s, b, part):
        return pair.at[s, b] if part is None else pair.at[s, b, part]

    def to_ring(n, direction, hop, b, part):
        s = streams[n][0]
        side = 0 if direction == 1 else 1
        ref = view(s, b, part)
        send(ref, ref, z_s.at[n, side, hop], z_r.at[n, side, hop], up if direction == 1 else down)

    def to_mate(s, side, slot, b, part):
        ref = view(s, b, part)
        send(ref, ref, p_s.at[s, side, slot], p_r.at[s, side, slot], mate)

    def to_far(s, slot, b, part):
        ref = view(s, b, part)
        send(ref, ref, f_s.at[s, slot], f_r.at[s, slot], far)

    def slot_of(direction, hop):
        return hop if direction == 1 else 4 + hop

    own_copies[0].wait()
    for d in range(1, OCC):
        arrived(pair.at[:, v, occ_from(d)], gat_r.at[d])
    for s in range(STEPS):
        to_far(s, 0, v, None)
    for n in (0, 2, 3):
        for direction in (1, -1):
            to_ring(n, direction, 1, v, None)
    for s in range(STEPS):
        to_mate(s, 0, 0, v, None)
    other = block_at(1, 0)
    for s in range(STEPS):
        arrived(view(s, other, None), f_r.at[s, 0])
        if s == 0:
            for direction in (1, -1):
                to_ring(1, direction, 1, other, None)
        to_mate(s, 1, 0, other, None)

    def ring_step(n, hop):
        s, side = streams[n]
        for direction in (1, -1):
            b = block_at(side, -direction * hop)
            part = half[direction] if hop == 4 else None
            arrived(view(s, b, part), z_r.at[n, 0 if direction == 1 else 1, hop])
            if hop < 4:
                to_ring(n, direction, hop + 1, b, half[direction] if hop == 3 else None)
            if s > 0:
                to_far(s, slot_of(direction, hop), b, part)
            to_mate(s, side, slot_of(direction, hop), b, part)

    def far_step(s, hop):
        for direction in (1, -1):
            b = block_at(1, -direction * hop)
            part = half[direction] if hop == 4 else None
            arrived(view(s, b, part), f_r.at[s, slot_of(direction, hop)])
            to_mate(s, 1, slot_of(direction, hop), b, part)

    def mate_done(s):
        for side in range(2):
            for slot in range(9):
                direction, hop = (1, slot) if slot <= 4 else (-1, slot - 4)
                b = block_at(side, -direction * hop) + 1 - 2 * core
                part = half[direction] if hop == 4 else None
                arrived(view(s, b, part), p_r.at[s, side, slot])

    def rows_done(c):
        own_copies[1 + c].wait()
        for u in range(2):
            for d in range(1, OCC):
                arrived(rows[c].at[occ_from(d), u], in_r.at[c, u, d])

    def integrals(c, s):
        sub = i_sub[s]
        column = er[s, pl.ds(c * M, M), :]
        column = jnp.concatenate([column] * (NB // 128), axis=1)

        def body(j, carry):
            left = jnp.concatenate([rows[c][r, sub].reshape(M, PB) for r in range(OCC)], axis=1)
            right = jnp.concatenate([pair[s, pl.ds(j * VB, VB), r].reshape(NB, PB) for r in range(OCC)], axis=1)
            value = lax.dot_general(left, right, (((1,), (1,)), ((), ())), preferred_element_type=F32)
            row = jnp.concatenate([e_vir[pl.ds(j * 2 + h, 1), :] for h in range(2)], axis=1)
            amp[j] = (-value / (column + row)).astype(BF16)
            return carry

        lax.fori_loop(0, JB, body, 0, unroll=2)

    def density(c, s):
        sub = i_sub[s]

        def body(d, carry):
            r = occ_at(d)
            left = jnp.concatenate([amp[j] for j in range(JB)], axis=1)
            value = jnp.dot(left, pair[s, :, r].reshape(VIR * AB, PB), preferred_element_type=F32)
            for u in range(2):
                term = jnp.where(sub == u, value, 0.0)
                if s == 0:
                    acc[u, d] = term
                elif s < STEPS - 1:
                    acc[u, d] = acc[u, d] + term
                else:
                    snd[c][d, u] = (acc[u, d] + term).astype(BF16).reshape(KB, AB, PB)
            return carry

        lax.fori_loop(0, OCC, body, 0, unroll=2)

    def send_out(c):
        for d in order:
            for u in range(2):
                send(snd[c].at[d, u], out.at[o, u, pl.ds(c * KB, KB)], o_s.at[c, u, d], o_r.at[c, u, d], (occ_at(d), v))
        copy = pltpu.make_async_copy(snd[c].at[0], out.at[o, :, pl.ds(c * KB, KB)], loc.at[3 + c])
        copy.start()
        return copy

    for hop in range(1, 5):
        ring_step(0, hop)
        ring_step(1, hop)
        if hop > 1:
            far_step(1, hop - 1)
        ring_step(2, hop)
        if hop > 1:
            far_step(2, hop - 1)
        ring_step(3, hop)
        if hop == 4:
            mate_done(0)
            rows_done(0)
            integrals(0, 0)
            density(0, 0)
    far_step(1, 4)
    far_step(2, 4)
    mate_done(1)
    integrals(0, 1)
    density(0, 1)
    mate_done(2)
    integrals(0, 2)
    density(0, 2)
    last = [send_out(0)]
    rows_done(1)
    for s in range(STEPS):
        integrals(1, s)
        density(1, s)
    last.append(send_out(1))
    for copy in last:
        copy.wait()
    for c in range(CHUNKS):
        for u in range(2):
            for d in range(1, OCC):
                arrived(out.at[occ_from(d), u, pl.ds(c * KB, KB)], o_r.at[c, u, d])
    for copy in sends:
        copy.wait_send()


def shards(factors, e_occ, e_vir, i_sub, j_row):
    own_pair = jnp.stack(
        [lax.dynamic_index_in_dim(factors, j_row[s], 0, keepdims=False) for s in range(STEPS)]
    )
    dma = pltpu.SemaphoreType.DMA
    smem, vmem, hbm = (pl.BlockSpec(memory_space=m) for m in (pltpu.SMEM, pltpu.VMEM, pl.ANY))
    result = pl.pallas_call(
        kernel,
        out_shape=jax.ShapeDtypeStruct((OCC, 2, IBK, AB, PB), BF16),
        in_specs=[smem, smem, smem, vmem, hbm, hbm],
        out_specs=hbm,
        scratch_shapes=[
            pltpu.VMEM((STEPS, VIR, OCC, AB, PB), BF16),
            pltpu.VMEM((OCC, 2, KB, AB, PB), BF16),
            pltpu.VMEM((OCC, 2, KB, AB, PB), BF16),
            pltpu.VMEM((STEPS, IBK * AB, 128), F32),
            pltpu.VMEM((JB, M, NB), BF16),
            pltpu.VMEM((2, OCC, M, PB), F32),
            pltpu.VMEM((OCC, 2, KB, AB, PB), BF16),
            pltpu.VMEM((OCC, 2, KB, AB, PB), BF16),
            dma((CHUNKS, 2, OCC)), dma((CHUNKS, 2, OCC)),
            dma((OCC,)), dma((OCC,)),
            dma((4, 2, 5)), dma((4, 2, 5)),
            dma((STEPS, 9)), dma((STEPS, 9)),
            dma((STEPS, 2, 9)), dma((STEPS, 2, 9)),
            dma((CHUNKS, 2, OCC)), dma((CHUNKS, 2, OCC)),
            dma((5,)),
        ],
        compiler_params=pltpu.CompilerParams(
            collective_id=0, has_side_effects=True, vmem_limit_bytes=48 * 2**20
        ),
        name="pair_densities",
    )(
        i_sub, j_row, e_occ, e_vir.reshape(8, 128),
        factors.reshape(OCC, 2, IBK, AB, PB), own_pair,
    )
    return result.reshape(factors.shape).astype(F32)


def solution(mesh):
    placed = (P(None, "vir", "occ"), P(), P(), P(), P())
    return jax.shard_map(
        shards, mesh=mesh, in_specs=placed, out_specs=P(None, "vir", "occ"), check_vma=False
    )
```

```python
import jax
import jax.numpy as jnp
from jax import lax
from jax.experimental import pallas as pl
from jax.experimental.pallas import tpu as pltpu
from jax.sharding import PartitionSpec as P

MESH = pl.DeviceIdType.MESH
F32 = jnp.float32
BF16 = jnp.bfloat16

STEPS = 3
IBK = 16
OCC = 8
VIR = 32
AB = 32
PB = 256
CHUNKS = 2
KB = IBK // CHUNKS
M = KB * AB
NB = 256
JB = VIR * AB // NB
FARTOP = 6


def rotate(index, shift, size):
    return lax.rem(index + (shift + size), size)


def kernel(
    i_sub_hbm, j_row_hbm, e_occ_hbm, e_vir_hbm, factors, out,
    i_sub, j_row, e_occ, e_vir, e_turned, e_group, er,
    held, own_pair, pair, rows0, rows1, amp, acc, snd0, snd1,
    in_s, in_r, gat_s, gat_r, z_s, z_r, f_s, f_r, p_s, p_r, o_s, o_r, loc,
):
    o, v = lax.axis_index("occ"), lax.axis_index("vir")
    yl, x = o // 4, lax.rem(o, 4)
    yh, z, core = v // 16, lax.rem(v // 2, 8), lax.rem(v, 2)
    rows, snd = (rows0, rows1), (snd0, snd1)

    def occ_at(d):
        return lax.rem(yl + d // 4, 2) * 4 + lax.rem(x + lax.rem(d, 4), 4)

    def occ_from(d):
        return lax.rem(yl + d // 4, 2) * 4 + lax.rem(x + 4 - lax.rem(d, 4), 4)

    def block_at(side, dz):
        high = 1 - yh if side else yh
        return high * 16 + rotate(z, dz, 8) * 2 + core

    far = ((1 - yl) * 4 + x, (1 - yh) * 16 + z * 2 + core)
    mate = (o, v + 1 - 2 * core)
    up = (o, block_at(0, 1))
    down = (o, block_at(0, -1))

    small = [
        pltpu.make_async_copy(a, b, loc.at[n])
        for n, (a, b) in enumerate(((j_row_hbm, j_row), (i_sub_hbm, i_sub), (e_occ_hbm, e_occ), (e_vir_hbm, e_vir)))
    ]
    small[0].start()
    whole = pltpu.make_async_copy(factors, held, loc.at[4])
    whole.start()
    for copy in small[1:]:
        copy.start()

    barrier = pltpu.get_barrier_semaphore()
    for d in range(1, OCC):
        pl.semaphore_signal(barrier, inc=1, device_id=(occ_at(d), v), device_id_type=MESH)
    for device in (far, mate, up, down):
        pl.semaphore_signal(barrier, inc=1, device_id=device, device_id_type=MESH)

    for copy in small:
        copy.wait()
    whole.wait()
    for s in range(STEPS):
        j = j_row[s]
        own_pair[s] = held[j // 32, lax.rem(j // 16, 2), lax.rem(j, 16)]
    pl.semaphore_wait(barrier, OCC + 3)

    sends = []

    def send(src, dst, ssem, rsem, device):
        copy = pltpu.make_async_remote_copy(
            src_ref=src, dst_ref=dst, send_sem=ssem, recv_sem=rsem, device_id=device, device_id_type=MESH
        )
        copy.start()
        sends.append(copy)

    def arrived(ref, rsem):
        pltpu.make_async_copy(ref, ref, rsem).wait()

    order = (1, 3, 4, 5, 7, 2, 6)
    for d in order:
        send(own_pair, pair.at[:, v, o], gat_s.at[d], gat_r.at[d], (occ_at(d), v))
    own_copies = [pltpu.make_async_copy(own_pair, pair.at[:, v, o], loc.at[5])]
    own_copies += [pltpu.make_async_copy(held.at[o, :, pl.ds(c * KB, KB)], rows[c].at[o], loc.at[6 + c]) for c in range(CHUNKS)]
    for copy in own_copies:
        copy.start()
    for c in range(CHUNKS):
        for u in range(2):
            for d in order:
                r = occ_at(d)
                send(factors.at[r, u, pl.ds(c * KB, KB)], rows[c].at[o, u], in_s.at[c, u, d], in_r.at[c, u, d], (r, v))

    e_turned[...] = pltpu.roll(e_vir[...], 64, 1)
    lanes = lax.broadcasted_iota(jnp.int32, (AB, 128), 1)
    subl = lax.broadcasted_iota(jnp.int32, (AB, 128), 0)
    mine = e_vir[pl.ds(v // 4, 1), :]
    own_e = jnp.sum(jnp.where(lanes == subl + lax.rem(v, 4) * AB, mine, 0.0), axis=1, keepdims=True)
    for s in range(STEPS):
        e_pair = e_occ[j_row[s]]
        first = o * 32 + i_sub[s] * IBK
        for k in range(IBK):
            er[s, k * AB : (k + 1) * AB, :] = jnp.broadcast_to(own_e - e_occ[first + k] - e_pair, (AB, 128))

    def places(g):
        return (z, rotate(z, 4, 8)) if g == 0 else (rotate(z, -g, 8), rotate(z, g, 8))

    lane = lax.broadcasted_iota(jnp.int32, (1, 128), 1)
    for g in range(JB):
        za, zb = places(g)
        for high in range(2):
            ra, rb = pl.ds(high * 4 + za // 2, 1), pl.ds(high * 4 + zb // 2, 1)
            ea = jnp.where(lax.rem(za, 2) == 0, e_vir[ra, :], e_turned[ra, :])
            eb = jnp.where(lax.rem(zb, 2) == 1, e_vir[rb, :], e_turned[rb, :])
            e_group[g, :, high * 128 : (high + 1) * 128] = jnp.where(lane < 64, ea, eb)

    streams = ((1, 0, 0, 8), (2, 0, 0, 8), (0, 0, 0, 8), (0, 1, 0, 8), (2, 1, FARTOP, 8))
    far_top = {0: 8, 1: 8, 2: FARTOP}

    def view(s, b, lo, hi):
        return pair.at[s, b] if (lo, hi) == (0, OCC) else pair.at[s, b, pl.ds(lo, hi - lo)]

    def part(direction, hop, lo, hi):
        if hop < 4:
            return lo, hi
        mid = (lo + hi) // 2
        return (lo, mid) if direction == 1 else (mid, hi)

    def to_ring(n, direction, hop, b):
        s, _, lo, hi = streams[n]
        side = 0 if direction == 1 else 1
        ref = view(s, b, *part(direction, hop, lo, hi))
        send(ref, ref, z_s.at[n, side, hop], z_r.at[n, side, hop], up if direction == 1 else down)

    def to_mate(kind, slot, s, b, lo, hi):
        ref = view(s, b, lo, hi)
        send(ref, ref, p_s.at[kind, slot], p_r.at[kind, slot], mate)

    def to_far(s, slot, b, lo, hi):
        hi = hi if slot == 0 else min(hi, far_top[s])
        if hi <= lo:
            return
        ref = view(s, b, lo, hi)
        send(ref, ref, f_s.at[s, slot], f_r.at[s, slot], far)

    def slot_of(direction, hop):
        return hop if direction == 1 else 4 + hop

    own_copies[0].wait()
    for d in range(1, OCC):
        arrived(pair.at[:, v, occ_from(d)], gat_r.at[d])
    for s in (0, 2, 1):
        to_far(s, 0, v, 0, 8)
    for n in range(3):
        for direction in (1, -1):
            to_ring(n, direction, 1, v)
    for n in range(3):
        to_mate(n, 0, streams[n][0], v, 0, 8)
    other = block_at(1, 0)
    for s, n in ((0, 3), (2, 4), (1, None)):
        arrived(view(s, other, 0, 8), f_r.at[s, 0])
        if n is not None:
            for direction in (1, -1):
                to_ring(n, direction, 1, other)
        to_mate(4 + s, 0, s, other, 0, 8)

    def ring_step(n, hop):
        s, side, lo, hi = streams[n]
        for direction in (1, -1):
            b = block_at(side, -direction * hop)
            slot = slot_of(direction, hop)
            p = part(direction, hop, lo, hi)
            arrived(view(s, b, *p), z_r.at[n, 0 if direction == 1 else 1, hop])
            if hop < 4:
                to_ring(n, direction, hop + 1, b)
            if s > 0 and side == 0:
                to_far(s, slot, b, *p)
            to_mate(7 if n == 4 else n, slot, s, b, *p)

    def far_step(s, hop):
        for direction in (1, -1):
            b = block_at(1, -direction * hop)
            slot = slot_of(direction, hop)
            lo, hi = part(direction, hop, 0, 8)
            hi = min(hi, far_top[s])
            if hi <= lo:
                continue
            arrived(view(s, b, lo, hi), f_r.at[s, slot])
            to_mate(4 + s, slot, s, b, lo, hi)

    def mate_done(kind, hops):
        s, side, lo, hi = streams[kind] if kind < 4 else (streams[4] if kind == 7 else (kind - 4, 1, 0, far_top[kind - 4]))
        for hop in hops:
            for direction in (1, -1) if hop else (1,):
                b = block_at(side, -direction * hop) + 1 - 2 * core
                p = part(direction, hop, lo, hi)
                if 4 <= kind < 7:
                    p = part(direction, hop, 0, 8)
                    p = (p[0], min(p[1], hi) if hop else 8)
                slot = slot_of(direction, hop)
                if p[0] < p[1]:
                    arrived(view(s, b, *p), p_r.at[kind, slot])

    def mate_all(s, hops):
        if s == 0:
            mate_done(2, hops)
            mate_done(3, [h for h in hops if h])
            mate_done(4, [h for h in hops if not h])
        else:
            mate_done(s - 1, hops)
            mate_done(4 + s, hops)
            if s == 2 and FARTOP < 8:
                mate_done(7, [h for h in hops if h])

    def rows_done(c):
        own_copies[1 + c].wait()
        for u in range(2):
            for d in range(1, OCC):
                arrived(rows[c].at[occ_from(d), u], in_r.at[c, u, d])

    def pieces(s, g, r):
        za, zb = places(g)
        return jnp.concatenate(
            [pair[s, pl.ds(high * 16 + zz * 2, 2), r].reshape(2 * AB, PB) for high in range(2) for zz in (za, zb)], axis=0
        )

    def integrals(c, s, g):
        column = er[s, pl.ds(c * M, M), :]
        column = jnp.concatenate([column] * (NB // 128), axis=1)
        sub = i_sub[s]
        left = jnp.concatenate([rows[c][r, sub].reshape(M, PB) for r in range(OCC)], axis=1)
        right = jnp.concatenate([pieces(s, g, r) for r in range(OCC)], axis=1)
        value = lax.dot_general(left, right, (((1,), (1,)), ((), ())), preferred_element_type=F32)
        amp[s, g] = (-value / (column + e_group[g])).astype(BF16)

    def density(c, s):
        sub = i_sub[s]

        def part_of(d):
            r = occ_at(d)
            left = jnp.concatenate([amp[s, g] for g in range(JB)], axis=1)
            right = jnp.concatenate([pieces(s, g, r) for g in range(JB)], axis=0)
            value = jnp.dot(left, right, preferred_element_type=F32)
            return [jnp.where(sub == u, value, 0.0) for u in range(2)]

        if s < STEPS - 1:
            def body(d, carry):
                for u, term in enumerate(part_of(d)):
                    acc[u, d] = term if s == 0 else acc[u, d] + term
                return carry

            lax.fori_loop(0, OCC, body, 0, unroll=4)
            return
        for d in order + (0,):
            for u, term in enumerate(part_of(d)):
                snd[c][d, u] = (acc[u, d] + term).astype(BF16).reshape(KB, AB, PB)
                if d:
                    send(snd[c].at[d, u], out.at[o, u, pl.ds(c * KB, KB)], o_s.at[c, u, d], o_r.at[c, u, d], (occ_at(d), v))
        last.append(pltpu.make_async_copy(snd[c].at[0], out.at[o, :, pl.ds(c * KB, KB)], loc.at[8 + c]))
        last[-1].start()

    last = []
    for hop in range(1, 5):
        for n in range(5 if FARTOP < 8 else 4):
            if n == 4 and hop > 1:
                far_step(1, hop - 1)
            ring_step(n, hop)
        if FARTOP == 8 and hop > 1:
            far_step(1, hop - 1)
        if hop > 1:
            far_step(2, hop - 1)
        if hop == 3:
            rows_done(0)
            mate_all(0, [1, 2])
            for s in (1, 2):
                mate_all(s, [1])
            for s, g in ((0, 1), (0, 2), (1, 1), (2, 1)):
                integrals(0, s, g)
    mate_all(0, [3])
    integrals(0, 0, 3)
    for s in (1, 2):
        mate_all(s, [2])
        integrals(0, s, 2)
    mate_all(0, [0, 4])
    integrals(0, 0, 0)
    far_step(1, 4)
    far_step(2, 4)
    density(0, 0)
    for s in (1, 2):
        mate_all(s, [3])
        integrals(0, s, 3)
        mate_all(s, [0, 4])
        integrals(0, s, 0)
        density(0, s)
    rows_done(1)
    for s in range(STEPS):
        for g in range(JB):
            integrals(1, s, g)
        density(1, s)
    for copy in last:
        copy.wait()
    for c in range(CHUNKS):
        for u in range(2):
            for d in range(1, OCC):
                arrived(out.at[occ_from(d), u, pl.ds(c * KB, KB)], o_r.at[c, u, d])
    for copy in sends:
        copy.wait_send()


def shards(factors, e_occ, e_vir, i_sub, j_row):
    dma = pltpu.SemaphoreType.DMA
    hbm = pl.BlockSpec(memory_space=pltpu.HBM)
    result = pl.pallas_call(
        kernel,
        out_shape=jax.ShapeDtypeStruct((OCC, 2, IBK, AB, PB), BF16),
        in_specs=[hbm] * 5,
        out_specs=pl.BlockSpec(memory_space=pl.ANY),
        scratch_shapes=[
            pltpu.SMEM((STEPS,), jnp.int32),
            pltpu.SMEM((STEPS,), jnp.int32),
            pltpu.SMEM((256,), F32),
            pltpu.VMEM((8, 128), F32),
            pltpu.VMEM((8, 128), F32),
            pltpu.VMEM((JB, 1, NB), F32),
            pltpu.VMEM((STEPS, IBK * AB, 128), F32),
            pltpu.VMEM((OCC, 2, IBK, AB, PB), BF16),
            pltpu.VMEM((STEPS, AB, PB), BF16),
            pltpu.VMEM((STEPS, VIR, OCC, AB, PB), BF16),
            pltpu.VMEM((OCC, 2, KB, AB, PB), BF16),
            pltpu.VMEM((OCC, 2, KB, AB, PB), BF16),
            pltpu.VMEM((STEPS, JB, M, NB), BF16),
            pltpu.VMEM((2, OCC, M, PB), F32),
            pltpu.VMEM((OCC, 2, KB, AB, PB), BF16),
            pltpu.VMEM((OCC, 2, KB, AB, PB), BF16),
            dma((CHUNKS, 2, OCC)), dma((CHUNKS, 2, OCC)),
            dma((OCC,)), dma((OCC,)),
            dma((5, 2, 5)), dma((5, 2, 5)),
            dma((STEPS, 9)), dma((STEPS, 9)),
            dma((8, 9)), dma((8, 9)),
            dma((CHUNKS, 2, OCC)), dma((CHUNKS, 2, OCC)),
            dma((10,)),
        ],
        compiler_params=pltpu.CompilerParams(
            collective_id=0, has_side_effects=True, vmem_limit_bytes=67_043_328
        ),
        name="pair_densities",
    )(i_sub, j_row, e_occ, e_vir.reshape(8, 128), factors.reshape(OCC, 2, IBK, AB, PB))
    return result.reshape(factors.shape).astype(F32)


def solution(mesh):
    placed = (P(None, "vir", "occ"), P(), P(), P(), P())
    return jax.shard_map(
        shards, mesh=mesh, in_specs=placed, out_specs=P(None, "vir", "occ"), check_vma=False
    )
```

```python
import jax
import jax.numpy as jnp
from jax import lax
from jax.experimental import pallas as pl
from jax.experimental.pallas import tpu as pltpu
from jax.sharding import PartitionSpec as P

MESH = pl.DeviceIdType.MESH
F32 = jnp.float32
BF16 = jnp.bfloat16

STEPS = 3
IBK = 16
OCC = 8
VIR = 32
AB = 32
PB = 256
CHUNKS = 2
KB = IBK // CHUNKS
M = KB * AB
NB = 256
JB = VIR * AB // NB
WIDE = 16
STEP_ORDER = (2, 0, 1)
FARTOP = 6


def rotate(index, shift, size):
    return lax.rem(index + (shift + size), size)


def kernel(
    i_sub_hbm, j_row_hbm, e_occ_hbm, e_vir_hbm, factors, out,
    i_sub, j_row, e_occ, e_vir, e_turned, e_group, er,
    held, own_pair, pair, rows0, rows1, amp, acc, snd0, snd1,
    in_s, in_r, gat_s, gat_r, z_s, z_r, f_s, f_r, p_s, p_r, o_s, o_r, loc,
):
    o, v = lax.axis_index("occ"), lax.axis_index("vir")
    yl, x = o // 4, lax.rem(o, 4)
    yh, z, core = v // 16, lax.rem(v // 2, 8), lax.rem(v, 2)
    rows, snd = (rows0, rows1), (snd0, snd1)

    def occ_at(d):
        return lax.rem(yl + d // 4, 2) * 4 + lax.rem(x + lax.rem(d, 4), 4)

    def occ_from(d):
        return lax.rem(yl + d // 4, 2) * 4 + lax.rem(x + 4 - lax.rem(d, 4), 4)

    def block_at(side, dz):
        high = 1 - yh if side else yh
        return high * 16 + rotate(z, dz, 8) * 2 + core

    far = ((1 - yl) * 4 + x, (1 - yh) * 16 + z * 2 + core)
    mate = (o, v + 1 - 2 * core)
    up = (o, block_at(0, 1))
    down = (o, block_at(0, -1))

    small = [
        pltpu.make_async_copy(a, b, loc.at[n])
        for n, (a, b) in enumerate(((j_row_hbm, j_row), (i_sub_hbm, i_sub), (e_occ_hbm, e_occ), (e_vir_hbm, e_vir)))
    ]
    small[0].start()
    whole = pltpu.make_async_copy(factors, held, loc.at[4])
    whole.start()
    for copy in small[1:]:
        copy.start()

    barrier = pltpu.get_barrier_semaphore()
    for d in range(1, OCC):
        pl.semaphore_signal(barrier, inc=1, device_id=(occ_at(d), v), device_id_type=MESH)
    for device in (far, mate, up, down):
        pl.semaphore_signal(barrier, inc=1, device_id=device, device_id_type=MESH)

    for copy in small:
        copy.wait()
    whole.wait()
    for s in range(STEPS):
        j = j_row[s]
        own_pair[s] = held[j // 32, lax.rem(j // 16, 2), lax.rem(j, 16)]
    pl.semaphore_wait(barrier, OCC + 3)

    sends = []

    def send(src, dst, ssem, rsem, device):
        copy = pltpu.make_async_remote_copy(
            src_ref=src, dst_ref=dst, send_sem=ssem, recv_sem=rsem, device_id=device, device_id_type=MESH
        )
        copy.start()
        sends.append(copy)

    def arrived(ref, rsem):
        pltpu.make_async_copy(ref, ref, rsem).wait()

    order = (1, 3, 4, 5, 7, 2, 6)
    for s in STEP_ORDER:
        for d in order:
            send(own_pair.at[s], pair.at[s, v, o], gat_s.at[s, d], gat_r.at[s, d], (occ_at(d), v))
    own_copies = [pltpu.make_async_copy(own_pair, pair.at[:, v, o], loc.at[5])]
    own_copies += [pltpu.make_async_copy(held.at[o, :, pl.ds(c * KB, KB)], rows[c].at[o], loc.at[6 + c]) for c in range(CHUNKS)]
    for copy in own_copies:
        copy.start()
    for c in range(CHUNKS):
        for u in range(2):
            for d in order:
                r = occ_at(d)
                send(factors.at[r, u, pl.ds(c * KB, KB)], rows[c].at[o, u], in_s.at[c, u, d], in_r.at[c, u, d], (r, v))

    e_turned[...] = pltpu.roll(e_vir[...], 64, 1)
    lanes = lax.broadcasted_iota(jnp.int32, (AB, 128), 1)
    subl = lax.broadcasted_iota(jnp.int32, (AB, 128), 0)
    mine = e_vir[pl.ds(v // 4, 1), :]
    own_e = jnp.sum(jnp.where(lanes == subl + lax.rem(v, 4) * AB, mine, 0.0), axis=1, keepdims=True)
    for s in range(STEPS):
        e_pair = e_occ[j_row[s]]
        first = o * 32 + i_sub[s] * IBK
        for k in range(IBK):
            er[s, k * AB : (k + 1) * AB, :] = jnp.broadcast_to(own_e - e_occ[first + k] - e_pair, (AB, 128))

    def places(g):
        return (z, rotate(z, 4, 8)) if g == 0 else (rotate(z, -g, 8), rotate(z, g, 8))

    lane = lax.broadcasted_iota(jnp.int32, (1, 128), 1)
    for g in range(JB):
        za, zb = places(g)
        for high in range(2):
            ra, rb = pl.ds(high * 4 + za // 2, 1), pl.ds(high * 4 + zb // 2, 1)
            ea = jnp.where(lax.rem(za, 2) == 0, e_vir[ra, :], e_turned[ra, :])
            eb = jnp.where(lax.rem(zb, 2) == 1, e_vir[rb, :], e_turned[rb, :])
            e_group[g, :, high * 128 : (high + 1) * 128] = jnp.where(lane < 64, ea, eb)

    streams = ((2, 0, 0, 8), (0, 0, 0, 8), (1, 0, 0, 8), (0, 1, 0, 8), (2, 1, FARTOP, 8))
    far_top = {0: 8, 1: 8, 2: FARTOP}

    def view(s, b, lo, hi):
        return pair.at[s, b] if (lo, hi) == (0, OCC) else pair.at[s, b, pl.ds(lo, hi - lo)]

    def part(direction, hop, lo, hi):
        if hop < 4:
            return lo, hi
        mid = (lo + hi) // 2
        return (lo, mid) if direction == 1 else (mid, hi)

    def to_ring(n, direction, hop, b):
        s, _, lo, hi = streams[n]
        side = 0 if direction == 1 else 1
        ref = view(s, b, *part(direction, hop, lo, hi))
        send(ref, ref, z_s.at[n, side, hop], z_r.at[n, side, hop], up if direction == 1 else down)

    def to_mate(kind, slot, s, b, lo, hi):
        ref = view(s, b, lo, hi)
        send(ref, ref, p_s.at[kind, slot], p_r.at[kind, slot], mate)

    def to_far(s, slot, b, lo, hi):
        hi = hi if slot == 0 else min(hi, far_top[s])
        if hi <= lo:
            return
        ref = view(s, b, lo, hi)
        send(ref, ref, f_s.at[s, slot], f_r.at[s, slot], far)

    def slot_of(direction, hop):
        return hop if direction == 1 else 4 + hop

    own_copies[0].wait()
    for n, s in enumerate(STEP_ORDER):
        for d in range(1, OCC):
            arrived(pair.at[s, v, occ_from(d)], gat_r.at[s, d])
        for direction in (1, -1):
            to_ring(n, direction, 1, v)
        to_far(s, 0, v, 0, 8)
        to_mate(n, 0, s, v, 0, 8)
    other = block_at(1, 0)
    for s, n in ((2, 4), (0, 3), (1, None)):
        arrived(view(s, other, 0, 8), f_r.at[s, 0])
        if n is not None:
            for direction in (1, -1):
                to_ring(n, direction, 1, other)
        to_mate(4 + s, 0, s, other, 0, 8)

    def ring_step(n, hop):
        s, side, lo, hi = streams[n]
        for direction in (1, -1):
            b = block_at(side, -direction * hop)
            slot = slot_of(direction, hop)
            p = part(direction, hop, lo, hi)
            arrived(view(s, b, *p), z_r.at[n, 0 if direction == 1 else 1, hop])
            if hop < 4:
                to_ring(n, direction, hop + 1, b)
            if s > 0 and side == 0:
                to_far(s, slot, b, *p)
            to_mate(7 if n == 4 else n, slot, s, b, *p)

    def far_step(s, hop):
        for direction in (1, -1):
            b = block_at(1, -direction * hop)
            slot = slot_of(direction, hop)
            lo, hi = part(direction, hop, 0, 8)
            hi = min(hi, far_top[s])
            if hi <= lo:
                continue
            arrived(view(s, b, lo, hi), f_r.at[s, slot])
            to_mate(4 + s, slot, s, b, lo, hi)

    def mate_done(kind, hops):
        s, side, lo, hi = streams[kind] if kind < 4 else (streams[4] if kind == 7 else (kind - 4, 1, 0, far_top[kind - 4]))
        for hop in hops:
            for direction in (1, -1) if hop else (1,):
                b = block_at(side, -direction * hop) + 1 - 2 * core
                p = part(direction, hop, lo, hi)
                if 4 <= kind < 7:
                    p = part(direction, hop, 0, 8)
                    p = (p[0], min(p[1], hi) if hop else 8)
                slot = slot_of(direction, hop)
                if p[0] < p[1]:
                    arrived(view(s, b, *p), p_r.at[kind, slot])

    def mate_all(s, hops):
        if s == 0:
            mate_done(1, hops)
            mate_done(3, [h for h in hops if h])
            mate_done(4, [h for h in hops if not h])
        else:
            mate_done(STEP_ORDER.index(s), hops)
            mate_done(4 + s, hops)
            if s == 2 and FARTOP < 8:
                mate_done(7, [h for h in hops if h])

    def rows_done(c):
        own_copies[1 + c].wait()
        for u in range(2):
            for d in range(1, OCC):
                arrived(rows[c].at[occ_from(d), u], in_r.at[c, u, d])

    def pieces(s, g, r):
        za, zb = places(g)
        return jnp.concatenate(
            [pair[s, pl.ds(high * 16 + zz * 2, 2), r].reshape(2 * AB, PB) for high in range(2) for zz in (za, zb)], axis=0
        )

    def integrals(c, s, g):
        column = er[s, pl.ds(c * M, M), :]
        column = jnp.concatenate([column] * (NB // 128), axis=1)
        sub = i_sub[s]
        left = jnp.concatenate([rows[c][r, sub].reshape(M, PB) for r in range(OCC)], axis=1)
        right = jnp.concatenate([pieces(s, g, r) for r in range(OCC)], axis=1)
        value = lax.dot_general(left, right, (((1,), (1,)), ((), ())), preferred_element_type=F32)
        amp[s, g] = (-value / (column + e_group[g])).astype(BF16)

    def terms(d, parts):
        r = occ_at(d)
        total = [None, None]
        for s, groups in parts:
            left = jnp.concatenate([amp[s, g] for g in groups], axis=1)
            right = jnp.concatenate([pieces(s, g, r) for g in groups], axis=0)
            value = jnp.dot(left, right, preferred_element_type=F32)
            for u in range(2):
                term = jnp.where(i_sub[s] == u, value, 0.0)
                total[u] = term if total[u] is None else total[u] + term
        return total

    def add(parts, first):
        def body(d, carry):
            for u, term in enumerate(terms(d, parts)):
                acc[u, d] = term if first else acc[u, d] + term
            return carry

        lax.fori_loop(0, OCC, body, 0, unroll=2)

    last = []

    def finish(c, parts, held_sum):
        for d in order + (0,):
            for u, term in enumerate(terms(d, parts)):
                value = acc[u, d] + term if held_sum else term
                snd[c][d, u] = value.astype(BF16).reshape(KB, AB, PB)
                if d:
                    send(snd[c].at[d, u], out.at[o, u, pl.ds(c * KB, KB)], o_s.at[c, u, d], o_r.at[c, u, d], (occ_at(d), v))
        last.append(pltpu.make_async_copy(snd[c].at[0], out.at[o, :, pl.ds(c * KB, KB)], loc.at[8 + c]))
        last[-1].start()

    for hop in range(1, 5):
        for n in range(5):
            if n == 4 and hop > 1:
                far_step(1, hop - 1)
            ring_step(n, hop)
        if hop > 1:
            far_step(2, hop - 1)
        if hop == 3:
            rows_done(0)
            mate_all(0, [1, 2])
            for s in (1, 2):
                mate_all(s, [1])
            for s, g in ((0, 1), (0, 2), (1, 1), (2, 1)):
                integrals(0, s, g)
            add([(0, (1, 2))], True)
    mate_all(0, [3])
    integrals(0, 0, 3)
    for s in (1, 2):
        mate_all(s, [2])
        integrals(0, s, 2)
    add([(1, (1, 2)), (2, (1, 2))], False)
    far_step(1, 4)
    far_step(2, 4)
    mate_all(0, [0, 4])
    integrals(0, 0, 0)
    for s in (1, 2):
        mate_all(s, [3])
        integrals(0, s, 3)
    add([(0, (3, 0))], False)
    for s in (1, 2):
        mate_all(s, [0, 4])
        integrals(0, s, 0)
    finish(0, [(1, (3, 0)), (2, (3, 0))], True)
    rows_done(1)
    for s in range(STEPS):
        for g in range(JB):
            integrals(1, s, g)
    finish(1, [(s, tuple(range(JB))) for s in range(STEPS)], False)
    for copy in last:
        copy.wait()
    for c in range(CHUNKS):
        for u in range(2):
            for d in range(1, OCC):
                arrived(out.at[occ_from(d), u, pl.ds(c * KB, KB)], o_r.at[c, u, d])
    for copy in sends:
        copy.wait_send()


def widen(source, out, narrow, wide, in_sem, out_sem):
    count = source.shape[0] // WIDE
    parts = [pl.ds(n * count, count) for n in range(WIDE)]
    ins = [pltpu.make_async_copy(source.at[p], narrow.at[p], in_sem.at[n]) for n, p in enumerate(parts)]
    outs = [pltpu.make_async_copy(wide.at[p], out.at[p], out_sem.at[n]) for n, p in enumerate(parts)]
    for copy in ins:
        copy.start()
    for n, p in enumerate(parts):
        ins[n].wait()
        wide[p] = narrow[p].astype(F32)
        outs[n].start()
    for copy in outs:
        copy.wait()


def shards(factors, e_occ, e_vir, i_sub, j_row):
    dma = pltpu.SemaphoreType.DMA
    hbm = pl.BlockSpec(memory_space=pltpu.HBM)
    result = pl.pallas_call(
        kernel,
        out_shape=jax.ShapeDtypeStruct((OCC, 2, IBK, AB, PB), BF16),
        in_specs=[hbm] * 5,
        out_specs=pl.BlockSpec(memory_space=pl.ANY),
        scratch_shapes=[
            pltpu.SMEM((STEPS,), jnp.int32),
            pltpu.SMEM((STEPS,), jnp.int32),
            pltpu.SMEM((256,), F32),
            pltpu.VMEM((8, 128), F32),
            pltpu.VMEM((8, 128), F32),
            pltpu.VMEM((JB, 1, NB), F32),
            pltpu.VMEM((STEPS, IBK * AB, 128), F32),
            pltpu.VMEM((OCC, 2, IBK, AB, PB), BF16),
            pltpu.VMEM((STEPS, AB, PB), BF16),
            pltpu.VMEM((STEPS, VIR, OCC, AB, PB), BF16),
            pltpu.VMEM((OCC, 2, KB, AB, PB), BF16),
            pltpu.VMEM((OCC, 2, KB, AB, PB), BF16),
            pltpu.VMEM((STEPS, JB, M, NB), BF16),
            pltpu.VMEM((2, OCC, M, PB), F32),
            pltpu.VMEM((OCC, 2, KB, AB, PB), BF16),
            pltpu.VMEM((OCC, 2, KB, AB, PB), BF16),
            dma((CHUNKS, 2, OCC)), dma((CHUNKS, 2, OCC)),
            dma((STEPS, OCC)), dma((STEPS, OCC)),
            dma((5, 2, 5)), dma((5, 2, 5)),
            dma((STEPS, 9)), dma((STEPS, 9)),
            dma((8, 9)), dma((8, 9)),
            dma((CHUNKS, 2, OCC)), dma((CHUNKS, 2, OCC)),
            dma((10,)),
        ],
        compiler_params=pltpu.CompilerParams(
            collective_id=0, has_side_effects=True, vmem_limit_bytes=67_043_328
        ),
        name="pair_densities",
    )(i_sub, j_row, e_occ, e_vir.reshape(8, 128), factors.reshape(OCC, 2, IBK, AB, PB))
    return pl.pallas_call(
        widen,
        out_shape=jax.ShapeDtypeStruct(factors.shape, F32),
        in_specs=[hbm],
        out_specs=hbm,
        scratch_shapes=[
            pltpu.VMEM(factors.shape, BF16),
            pltpu.VMEM(factors.shape, F32),
            dma((WIDE,)), dma((WIDE,)),
        ],
        compiler_params=pltpu.CompilerParams(vmem_limit_bytes=67_043_328),
        name="widen",
    )(result.reshape(factors.shape))


def solution(mesh):
    placed = (P(None, "vir", "occ"), P(), P(), P(), P())
    return jax.shard_map(
        shards, mesh=mesh, in_specs=placed, out_specs=P(None, "vir", "occ"), check_vma=False
    )
```

```python
import jax
import jax.numpy as jnp
from jax import lax
from jax.experimental import pallas as pl
from jax.experimental.pallas import tpu as pltpu
from jax.sharding import PartitionSpec as P

MESH = pl.DeviceIdType.MESH
F32 = jnp.float32
BF16 = jnp.bfloat16

STEPS = 3
IBK = 16
OCC = 8
VIR = 32
AB = 32
PB = 256
CHUNKS = 2
KB = IBK // CHUNKS
M = KB * AB
NB = 256
JB = VIR * AB // NB
WIDE = 16
STEP_ORDER = (2, 0, 1)
FARTOP = 6


def rotate(index, shift, size):
    return lax.rem(index + (shift + size), size)


def kernel(
    i_sub_hbm, j_row_hbm, e_occ_hbm, e_vir_hbm, factors, out,
    i_sub, j_row, e_occ, e_vir, e_turned, e_group, er,
    held, own_pair, pair, rows0, rows1, amp, acc, snd0, snd1,
    in_s, in_r, gat_s, gat_r, z_s, z_r, f_s, f_r, p_s, p_r, o_s, o_r, loc,
):
    o, v = lax.axis_index("occ"), lax.axis_index("vir")
    yl, x = o // 4, lax.rem(o, 4)
    yh, z, core = v // 16, lax.rem(v // 2, 8), lax.rem(v, 2)
    rows, snd = (rows0, rows1), (snd0, snd1)

    def occ_at(d):
        return lax.rem(yl + d // 4, 2) * 4 + lax.rem(x + lax.rem(d, 4), 4)

    def occ_from(d):
        return lax.rem(yl + d // 4, 2) * 4 + lax.rem(x + 4 - lax.rem(d, 4), 4)

    def block_at(side, dz):
        high = 1 - yh if side else yh
        return high * 16 + rotate(z, dz, 8) * 2 + core

    far = ((1 - yl) * 4 + x, (1 - yh) * 16 + z * 2 + core)
    mate = (o, v + 1 - 2 * core)
    up = (o, block_at(0, 1))
    down = (o, block_at(0, -1))

    small = [
        pltpu.make_async_copy(a, b, loc.at[n])
        for n, (a, b) in enumerate(((j_row_hbm, j_row), (i_sub_hbm, i_sub), (e_occ_hbm, e_occ), (e_vir_hbm, e_vir)))
    ]
    small[0].start()
    whole = pltpu.make_async_copy(factors, held, loc.at[4])
    whole.start()
    for copy in small[1:]:
        copy.start()

    barrier = pltpu.get_barrier_semaphore()
    for d in range(1, OCC):
        pl.semaphore_signal(barrier, inc=1, device_id=(occ_at(d), v), device_id_type=MESH)
    for device in (far, mate, up, down):
        pl.semaphore_signal(barrier, inc=1, device_id=device, device_id_type=MESH)

    for copy in small:
        copy.wait()
    whole.wait()
    for s in range(STEPS):
        j = j_row[s]
        own_pair[s] = held[j // 32, lax.rem(j // 16, 2), lax.rem(j, 16)]
    pl.semaphore_wait(barrier, OCC + 3)

    sends = []

    def send(src, dst, ssem, rsem, device):
        copy = pltpu.make_async_remote_copy(
            src_ref=src, dst_ref=dst, send_sem=ssem, recv_sem=rsem, device_id=device, device_id_type=MESH
        )
        copy.start()
        sends.append(copy)

    def arrived(ref, rsem):
        pltpu.make_async_copy(ref, ref, rsem).wait()

    order = (1, 3, 4, 5, 7, 2, 6)
    for s in STEP_ORDER:
        for d in order:
            send(own_pair.at[s], pair.at[s, v, o], gat_s.at[s, d], gat_r.at[s, d], (occ_at(d), v))
    own_copies = [pltpu.make_async_copy(own_pair, pair.at[:, v, o], loc.at[5])]
    own_copies += [pltpu.make_async_copy(held.at[o, :, pl.ds(c * KB, KB)], rows[c].at[o], loc.at[6 + c]) for c in range(CHUNKS)]
    for copy in own_copies:
        copy.start()
    for c in range(CHUNKS):
        for u in range(2):
            for d in order:
                r = occ_at(d)
                send(factors.at[r, u, pl.ds(c * KB, KB)], rows[c].at[o, u], in_s.at[c, u, d], in_r.at[c, u, d], (r, v))

    e_turned[...] = pltpu.roll(e_vir[...], 64, 1)
    lanes = lax.broadcasted_iota(jnp.int32, (AB, 128), 1)
    subl = lax.broadcasted_iota(jnp.int32, (AB, 128), 0)
    mine = e_vir[pl.ds(v // 4, 1), :]
    own_e = jnp.sum(jnp.where(lanes == subl + lax.rem(v, 4) * AB, mine, 0.0), axis=1, keepdims=True)
    for s in range(STEPS):
        e_pair = e_occ[j_row[s]]
        first = o * 32 + i_sub[s] * IBK
        for k in range(IBK):
            er[s, k * AB : (k + 1) * AB, :] = jnp.broadcast_to(own_e - e_occ[first + k] - e_pair, (AB, 128))

    def places(g):
        return (z, rotate(z, 4, 8)) if g == 0 else (rotate(z, -g, 8), rotate(z, g, 8))

    lane = lax.broadcasted_iota(jnp.int32, (1, 128), 1)
    for g in range(JB):
        za, zb = places(g)
        for high in range(2):
            ra, rb = pl.ds(high * 4 + za // 2, 1), pl.ds(high * 4 + zb // 2, 1)
            ea = jnp.where(lax.rem(za, 2) == 0, e_vir[ra, :], e_turned[ra, :])
            eb = jnp.where(lax.rem(zb, 2) == 1, e_vir[rb, :], e_turned[rb, :])
            e_group[g, :, high * 128 : (high + 1) * 128] = jnp.where(lane < 64, ea, eb)

    streams = ((2, 0, 0, 8), (0, 0, 0, 8), (1, 0, 0, 8), (0, 1, 0, 8), (2, 1, FARTOP, 8))
    far_top = {0: 8, 1: 8, 2: FARTOP}

    def view(s, b, lo, hi):
        return pair.at[s, b] if (lo, hi) == (0, OCC) else pair.at[s, b, pl.ds(lo, hi - lo)]

    def part(direction, hop, lo, hi):
        if hop < 4:
            return lo, hi
        mid = (lo + hi) // 2
        return (lo, mid) if direction == 1 else (mid, hi)

    def to_ring(n, direction, hop, b):
        s, _, lo, hi = streams[n]
        side = 0 if direction == 1 else 1
        ref = view(s, b, *part(direction, hop, lo, hi))
        send(ref, ref, z_s.at[n, side, hop], z_r.at[n, side, hop], up if direction == 1 else down)

    def to_mate(kind, slot, s, b, lo, hi):
        ref = view(s, b, lo, hi)
        send(ref, ref, p_s.at[kind, slot], p_r.at[kind, slot], mate)

    def to_far(s, slot, b, lo, hi):
        hi = hi if slot == 0 else min(hi, far_top[s])
        if hi <= lo:
            return
        ref = view(s, b, lo, hi)
        send(ref, ref, f_s.at[s, slot], f_r.at[s, slot], far)

    def slot_of(direction, hop):
        return hop if direction == 1 else 4 + hop

    own_copies[0].wait()
    for n, s in enumerate(STEP_ORDER):
        for d in range(1, OCC):
            arrived(pair.at[s, v, occ_from(d)], gat_r.at[s, d])
        for direction in (1, -1):
            to_ring(n, direction, 1, v)
        to_far(s, 0, v, 0, 8)
        to_mate(n, 0, s, v, 0, 8)
    other = block_at(1, 0)
    for s, n in ((2, 4), (0, 3), (1, None)):
        arrived(view(s, other, 0, 8), f_r.at[s, 0])
        if n is not None:
            for direction in (1, -1):
                to_ring(n, direction, 1, other)
        to_mate(4 + s, 0, s, other, 0, 8)

    def ring_step(n, hop):
        s, side, lo, hi = streams[n]
        for direction in (1, -1):
            b = block_at(side, -direction * hop)
            slot = slot_of(direction, hop)
            p = part(direction, hop, lo, hi)
            arrived(view(s, b, *p), z_r.at[n, 0 if direction == 1 else 1, hop])
            if hop < 4:
                to_ring(n, direction, hop + 1, b)
            if s > 0 and side == 0:
                to_far(s, slot, b, *p)
            to_mate(7 if n == 4 else n, slot, s, b, *p)

    def far_step(s, hop):
        for direction in (1, -1):
            b = block_at(1, -direction * hop)
            slot = slot_of(direction, hop)
            lo, hi = part(direction, hop, 0, 8)
            hi = min(hi, far_top[s])
            if hi <= lo:
                continue
            arrived(view(s, b, lo, hi), f_r.at[s, slot])
            to_mate(4 + s, slot, s, b, lo, hi)

    def mate_done(kind, hops):
        s, side, lo, hi = streams[kind] if kind < 4 else (streams[4] if kind == 7 else (kind - 4, 1, 0, far_top[kind - 4]))
        for hop in hops:
            for direction in (1, -1) if hop else (1,):
                b = block_at(side, -direction * hop) + 1 - 2 * core
                p = part(direction, hop, lo, hi)
                if 4 <= kind < 7:
                    p = part(direction, hop, 0, 8)
                    p = (p[0], min(p[1], hi) if hop else 8)
                slot = slot_of(direction, hop)
                if p[0] < p[1]:
                    arrived(view(s, b, *p), p_r.at[kind, slot])

    def mate_all(s, hops):
        if s == 0:
            mate_done(1, hops)
            mate_done(3, [h for h in hops if h])
            mate_done(4, [h for h in hops if not h])
        else:
            mate_done(STEP_ORDER.index(s), hops)
            mate_done(4 + s, hops)
            if s == 2 and FARTOP < 8:
                mate_done(7, [h for h in hops if h])

    def rows_done(c):
        own_copies[1 + c].wait()
        for u in range(2):
            for d in range(1, OCC):
                arrived(rows[c].at[occ_from(d), u], in_r.at[c, u, d])

    def pieces(s, g, r):
        za, zb = places(g)
        return jnp.concatenate(
            [pair[s, pl.ds(high * 16 + zz * 2, 2), r].reshape(2 * AB, PB) for high in range(2) for zz in (za, zb)], axis=0
        )

    def integrals(c, s, g):
        column = er[s, pl.ds(c * M, M), :]
        column = jnp.concatenate([column] * (NB // 128), axis=1)
        sub = i_sub[s]
        left = jnp.concatenate([rows[c][r, sub].reshape(M, PB) for r in range(OCC)], axis=1)
        right = jnp.concatenate([pieces(s, g, r) for r in range(OCC)], axis=1)
        value = lax.dot_general(left, right, (((1,), (1,)), ((), ())), preferred_element_type=F32)
        amp[s, g] = (-value / (column + e_group[g])).astype(BF16)

    def terms(d, parts):
        r = occ_at(d)
        total = [None, None]
        for s, groups in parts:
            left = jnp.concatenate([amp[s, g] for g in groups], axis=1)
            right = jnp.concatenate([pieces(s, g, r) for g in groups], axis=0)
            value = jnp.dot(left, right, preferred_element_type=F32)
            for u in range(2):
                term = jnp.where(i_sub[s] == u, value, 0.0)
                total[u] = term if total[u] is None else total[u] + term
        return total

    def add(parts, first):
        def body(d, carry):
            for u, term in enumerate(terms(d, parts)):
                acc[u, d] = term if first else acc[u, d] + term
            return carry

        lax.fori_loop(0, OCC, body, 0, unroll=2)

    last = []

    def finish(c, parts, held_sum):
        for d in order + (0,):
            for u, term in enumerate(terms(d, parts)):
                value = acc[u, d] + term if held_sum else term
                snd[c][d, u] = value.astype(BF16).reshape(KB, AB, PB)
                if d:
                    send(snd[c].at[d, u], out.at[o, u, pl.ds(c * KB, KB)], o_s.at[c, u, d], o_r.at[c, u, d], (occ_at(d), v))
        last.append(pltpu.make_async_copy(snd[c].at[0], out.at[o, :, pl.ds(c * KB, KB)], loc.at[8 + c]))
        last[-1].start()

    for hop in range(1, 5):
        for n in range(5):
            if n == 4 and hop > 1:
                far_step(1, hop - 1)
            ring_step(n, hop)
        if hop > 1:
            far_step(2, hop - 1)
        if hop == 3:
            rows_done(0)
            mate_all(0, [1, 2])
            for s in (1, 2):
                mate_all(s, [1])
            for s, g in ((0, 1), (0, 2), (1, 1), (2, 1)):
                integrals(0, s, g)
            add([(0, (1, 2))], True)
    mate_all(0, [3])
    integrals(0, 0, 3)
    for s in (1, 2):
        mate_all(s, [2])
        integrals(0, s, 2)
    add([(1, (1, 2)), (2, (1, 2))], False)
    far_step(1, 4)
    far_step(2, 4)
    mate_all(0, [0, 4])
    integrals(0, 0, 0)
    for s in (1, 2):
        mate_all(s, [3])
        integrals(0, s, 3)
    add([(0, (3, 0))], False)
    for s in (1, 2):
        mate_all(s, [0, 4])
        integrals(0, s, 0)
    gathered, returned = len(sends), 2 * (OCC - 1)
    finish(0, [(1, (3, 0)), (2, (3, 0))], True)
    rows_done(1)
    for s in range(STEPS):
        for g in range(JB):
            integrals(1, s, g)
    finish(1, [(s, tuple(range(JB))) for s in range(STEPS)], False)
    for copy in sends[:gathered]:
        copy.wait_send()
    for copy in last:
        copy.wait()
    for c in range(CHUNKS):
        for copy in sends[gathered + c * returned : gathered + (c + 1) * returned]:
            copy.wait_send()
        for u in range(2):
            for d in range(1, OCC):
                arrived(out.at[occ_from(d), u, pl.ds(c * KB, KB)], o_r.at[c, u, d])


def widen(source, out, narrow, wide, in_sem, out_sem):
    count = source.shape[0] // WIDE
    parts = [pl.ds(n * count, count) for n in range(WIDE)]
    ins = [pltpu.make_async_copy(source.at[p], narrow.at[p], in_sem.at[n]) for n, p in enumerate(parts)]
    outs = [pltpu.make_async_copy(wide.at[p], out.at[p], out_sem.at[n]) for n, p in enumerate(parts)]
    for copy in ins:
        copy.start()
    for n, p in enumerate(parts):
        ins[n].wait()
        wide[p] = narrow[p].astype(F32)
        outs[n].start()
    for copy in outs:
        copy.wait()


def shards(factors, e_occ, e_vir, i_sub, j_row):
    dma = pltpu.SemaphoreType.DMA
    hbm = pl.BlockSpec(memory_space=pltpu.HBM)
    result = pl.pallas_call(
        kernel,
        out_shape=jax.ShapeDtypeStruct((OCC, 2, IBK, AB, PB), BF16),
        in_specs=[hbm] * 5,
        out_specs=pl.BlockSpec(memory_space=pl.ANY),
        scratch_shapes=[
            pltpu.SMEM((STEPS,), jnp.int32),
            pltpu.SMEM((STEPS,), jnp.int32),
            pltpu.SMEM((256,), F32),
            pltpu.VMEM((8, 128), F32),
            pltpu.VMEM((8, 128), F32),
            pltpu.VMEM((JB, 1, NB), F32),
            pltpu.VMEM((STEPS, IBK * AB, 128), F32),
            pltpu.VMEM((OCC, 2, IBK, AB, PB), BF16),
            pltpu.VMEM((STEPS, AB, PB), BF16),
            pltpu.VMEM((STEPS, VIR, OCC, AB, PB), BF16),
            pltpu.VMEM((OCC, 2, KB, AB, PB), BF16),
            pltpu.VMEM((OCC, 2, KB, AB, PB), BF16),
            pltpu.VMEM((STEPS, JB, M, NB), BF16),
            pltpu.VMEM((2, OCC, M, PB), F32),
            pltpu.VMEM((OCC, 2, KB, AB, PB), BF16),
            pltpu.VMEM((OCC, 2, KB, AB, PB), BF16),
            dma((CHUNKS, 2, OCC)), dma((CHUNKS, 2, OCC)),
            dma((STEPS, OCC)), dma((STEPS, OCC)),
            dma((5, 2, 5)), dma((5, 2, 5)),
            dma((STEPS, 9)), dma((STEPS, 9)),
            dma((8, 9)), dma((8, 9)),
            dma((CHUNKS, 2, OCC)), dma((CHUNKS, 2, OCC)),
            dma((10,)),
        ],
        compiler_params=pltpu.CompilerParams(
            collective_id=0, has_side_effects=True, vmem_limit_bytes=67_043_328
        ),
        name="pair_densities",
    )(i_sub, j_row, e_occ, e_vir.reshape(8, 128), factors.reshape(OCC, 2, IBK, AB, PB))
    return pl.pallas_call(
        widen,
        out_shape=jax.ShapeDtypeStruct(factors.shape, F32),
        in_specs=[hbm],
        out_specs=hbm,
        scratch_shapes=[
            pltpu.VMEM(factors.shape, BF16),
            pltpu.VMEM(factors.shape, F32),
            dma((WIDE,)), dma((WIDE,)),
        ],
        compiler_params=pltpu.CompilerParams(vmem_limit_bytes=67_043_328),
        name="widen",
    )(result.reshape(factors.shape))


def solution(mesh):
    placed = (P(None, "vir", "occ"), P(), P(), P(), P())
    return jax.shard_map(
        shards, mesh=mesh, in_specs=placed, out_specs=P(None, "vir", "occ"), check_vma=False
    )
```
